32 devices in a mesh: ctx: 8 (over z, y), ch: 4 (over x, core).
Axes of the slice: x: 2, y: 2, z: 4, core: 2. Of those that a mesh axis runs over, the one named last changes fastest.
Arguments:
- tokens: bfloat16 [8192, 1536], P('ctx', 'ch'), may hold values from -6 to 6
- block_first: bfloat16 [16, 512, 512], P('ctx'), may hold values from -0.25 to 0.25
- block_second: bfloat16 [512, 16, 16], P('ctx'), may hold values from -1.5 to 1.5
- gate_weight: bfloat16 [1536, 1536], P(None, 'ch'), may hold values from -0.15625 to 0.15625
- conv_taps: float32 [4, 1536], P(None, 'ch'), may hold values from -3 to 3
- cotangent: bfloat16 [8192, 1536], P('ctx', 'ch'), may hold values from -6 to 6
Outputs:
- mixed_out: bfloat16 [8192, 1536], P('ctx', 'ch')
- grad_tokens: bfloat16 [8192, 1536], P('ctx', 'ch')
- grad_taps: float32 [4, 1536], P(None, 'ch')
- grad_gate_weight: float32 [1536, 1536], P(None, 'ch')
- grad_first: float32 [16, 512, 512], P('ctx')
- grad_second: float32 [512, 16, 16], P('ctx')
The draws below stay inside these ranges and needn't reach their ends.
All inputs are finite; a program needn't handle non-finite values.
Results may differ from the reference program's by a relative error of at most 0.0064.
Values may be sent and summed in bfloat16 or wider, within the bound.
No kernel may reach another device: no remote copies, remote signals or barrier semaphores. Data moves between devices by JAX's collectives and lax.ppermute only.
A program may use at most 64 MiB of HBM per device.

```python
import jax
import jax.numpy as jnp

D = 1536
BS = 512
TAPS = 4
NB = 16
TOKENS = 8192


def shard_levels(stream_key, extent, pieces, low, largest):
    def one(axis_at, blocks):
        heights = jax.random.uniform(jax.random.fold_in(jax.random.fold_in(stream_key, 6), axis_at), (blocks,), jnp.float32, low / len(pieces), largest / len(pieces))
        return jnp.repeat(jnp.exp(heights), extent[axis_at] // blocks).reshape((-1,) + (1,) * (len(extent) - axis_at - 1))

    factor_of = one(*pieces[0])
    for cut in pieces[1:]:
        factor_of = factor_of * one(*cut)
    return factor_of


def bell_draw(stream_key, dims, width, reach, shards=(), held_as=jnp.bfloat16):
    result = jax.random.normal(stream_key, dims, jnp.float32) * width
    if len(shards) > 0:
        result = shard_levels(stream_key, dims, shards, -0.22, 0.18) * result
    return jnp.clip(result, min=-reach, max=reach).astype(held_as)


def setup_inputs(seed: int = 0) -> dict:
    splits = jax.random.split(jax.random.key(seed), 7)
    tokens = bell_draw(splits[0], (TOKENS, D), 1.0, 6.0, ((0, 8), (1, 4)))
    block_first = bell_draw(splits[1], (NB, BS, BS), BS ** -0.5, 0.25, ((0, 8),))
    block_second = bell_draw(splits[2], (BS, NB, NB), NB ** -0.5, 1.5, ((0, 8),))
    gate_weight = bell_draw(splits[3], (D, D), D ** -0.5, 0.15625, ((1, 4),))
    conv_taps = bell_draw(splits[4], (TAPS, D), TAPS ** -0.5, 3.0, ((1, 4),), jnp.float32)
    cotangent = bell_draw(splits[5], (TOKENS, D), 1.0, 6.0, ((0, 8), (1, 4)))
    return dict(tokens=tokens, block_first=block_first, block_second=block_second, gate_weight=gate_weight, conv_taps=conv_taps, cotangent=cotangent)


def reference(tokens, block_first, block_second, gate_weight, conv_taps, cotangent):
    local_wide = tokens.astype(jnp.float32).reshape(NB, BS, D)
    first_out = jnp.einsum("nrs,nsc->nrc", block_first.astype(jnp.float32), local_wide).astype(jnp.bfloat16)
    first_wide = first_out.astype(jnp.float32)
    second_wide = block_second.astype(jnp.float32)
    second_out = jnp.einsum("rmn,nrc->mrc", second_wide, first_wide).astype(jnp.bfloat16)
    mixed_seq = second_out.reshape(TOKENS, D)
    gate_pre = jnp.dot(tokens, gate_weight, preferred_element_type=jnp.float32)
    gate_sig = jax.nn.sigmoid(gate_pre)
    mixed_wide = mixed_seq.astype(jnp.float32)
    gated_vals = (mixed_wide * gate_sig).astype(jnp.bfloat16)
    padded = jnp.concatenate([jnp.zeros((TAPS - 1, D), jnp.float32), gated_vals.astype(jnp.float32)], 0)
    conv_out = jnp.zeros((TOKENS, D), jnp.float32)
    for offset in range(TAPS):
        conv_out = conv_out + conv_taps[offset][None, :] * padded[TAPS - 1 - offset:TAPS - 1 - offset + TOKENS]
    mixed_out = conv_out.astype(jnp.bfloat16)
    cot_wide = cotangent.astype(jnp.float32)
    cot_pad = jnp.concatenate([cot_wide, jnp.zeros((TAPS - 1, D), jnp.float32)], 0)
    grad_gated = jnp.zeros((TOKENS, D), jnp.float32)
    tap_rows = []
    for offset in range(TAPS):
        grad_gated = grad_gated + conv_taps[offset][None, :] * cot_pad[offset:offset + TOKENS]
        tap_rows.append(jnp.sum(cot_wide * padded[TAPS - 1 - offset:TAPS - 1 - offset + TOKENS], 0))
    grad_taps = jnp.stack(tap_rows, 0)
    grad_mix = (grad_gated * gate_sig).astype(jnp.bfloat16)
    grad_gate = (grad_gated * mixed_wide * gate_sig * (1.0 - gate_sig)).astype(jnp.bfloat16)
    grad_gate_weight = jnp.dot(tokens.T, grad_gate, preferred_element_type=jnp.float32)
    gate_input_grad = jnp.dot(grad_gate, gate_weight.T, preferred_element_type=jnp.float32)
    grad_cols = grad_mix.astype(jnp.float32).reshape(NB, BS, D)
    grad_second = jnp.einsum("mrc,nrc->rmn", grad_cols, first_wide)
    grad_first_t = jnp.einsum("rmn,mrc->nrc", second_wide, grad_cols).astype(jnp.bfloat16)
    first_grad_wide = grad_first_t.astype(jnp.float32)
    grad_first = jnp.einsum("nrc,nsc->nrs", first_grad_wide, local_wide)
    grad_local = jnp.einsum("nrs,nrc->nsc", block_first.astype(jnp.float32), first_grad_wide).reshape(TOKENS, D)
    grad_tokens = (grad_local + gate_input_grad).astype(jnp.bfloat16)
    return (mixed_out, grad_tokens, grad_taps, grad_gate_weight, grad_first, grad_second)
```

```python
import jax
import jax.numpy as jnp
from jax import lax
from jax.sharding import PartitionSpec as P

BF = jnp.bfloat16
F32 = jnp.float32


def passed_along(array, axis, by):
    count = lax.axis_size(axis)
    pairs = [(i, i + by) for i in range(count) if 0 <= i + by < count]
    return lax.ppermute(array, axis, pairs)


def swap(array, axis, bit):
    count = lax.axis_size(axis)
    return lax.ppermute(array, axis, [(i, i ^ bit) for i in range(count)])


def pick(stacked, index):
    return lax.dynamic_index_in_dim(stacked, index, 0, keepdims=False)


def hi_lo(x):
    hi = x.astype(BF)
    lo = (x - hi.astype(F32)).astype(BF)
    return hi, lo


def on_device(tokens, block_first, block_second, gate_weight, conv_taps, cotangent):
    blocks, block_size, _ = block_first.shape
    tok_rows, chan_count = tokens.shape
    tap_count = conv_taps.shape[0]
    halo = tap_count - 1
    ch_count = lax.axis_size("ch")
    ctx_count = lax.axis_size("ctx")
    ch_at = lax.axis_index("ch")
    ctx_at = lax.axis_index("ctx")

    feats = [tokens]
    bit = ch_count // 2
    order = [0]
    while bit:
        got = [swap(f, "ch", bit) for f in feats]
        order = order + [o ^ bit for o in order]
        feats = feats + got
        bit //= 2
    w_blocks = gate_weight.reshape(ch_count, chan_count, chan_count)
    w_rel = [pick(w_blocks, ch_at ^ o) for o in order]

    local_blocks = tokens.reshape(blocks, block_size, chan_count)
    first_out = jnp.einsum(
        "nrs,nsc->nrc", block_first, local_blocks, preferred_element_type=F32
    ).astype(BF)
    columns = lax.all_to_all(first_out, "ctx", split_axis=1, concat_axis=0, tiled=True)
    second_out = jnp.einsum(
        "rmn,nrc->mrc", block_second, columns, preferred_element_type=F32
    ).astype(BF)
    mixed_seq = lax.all_to_all(second_out, "ctx", split_axis=0, concat_axis=1, tiled=True).reshape(
        tok_rows, chan_count
    )

    following = passed_along(cotangent[:halo], "ctx", -1)
    cot_wide = cotangent.astype(F32)
    cot_pad = jnp.concatenate([cotangent, following], 0).astype(F32)
    grad_gated = jnp.zeros((tok_rows, chan_count), F32)
    for offset in range(tap_count):
        grad_gated = grad_gated + conv_taps[offset][None, :] * cot_pad[offset : offset + tok_rows]

    gate_pre = jnp.zeros((tok_rows, chan_count), F32)
    for f, w in zip(feats, w_rel):
        gate_pre = gate_pre + jnp.dot(f, w, preferred_element_type=F32)
    gate_sig = jax.nn.sigmoid(gate_pre)
    grad_mix = (grad_gated * gate_sig).astype(BF)
    grad_cols = lax.all_to_all(
        grad_mix.reshape(blocks, block_size, chan_count),
        "ctx",
        split_axis=1,
        concat_axis=0,
        tiled=True,
    )

    mixed_wide = mixed_seq.astype(F32)
    gated_vals = (mixed_wide * gate_sig).astype(BF)
    grad_gate = (grad_gated * mixed_wide * gate_sig * (1.0 - gate_sig)).astype(BF)
    earlier = passed_along(gated_vals[tok_rows - halo :], "ctx", 1)
    padded = jnp.concatenate([earlier, gated_vals], 0).astype(F32)
    conv_out = jnp.zeros((tok_rows, chan_count), F32)
    tap_rows = []
    for offset in range(tap_count):
        window = padded[halo - offset : halo - offset + tok_rows]
        conv_out = conv_out + conv_taps[offset][None, :] * window
        tap_rows.append(jnp.sum(cot_wide * window, 0))
    mixed_out = conv_out.astype(BF)
    taps_sum = jnp.stack(tap_rows, 0)

    weight = [
        lax.dot_general(f, grad_gate, (((0,), (0,)), ((), ())), preferred_element_type=F32)
        for f in feats
    ]
    weight = jnp.concatenate(weight, 0)
    bit = 1
    halved = []
    while bit < ctx_count:
        last = bit * 2 >= ctx_count
        hi, lo = hi_lo(taps_sum)
        pad = jnp.zeros((16 - 2 * tap_count, chan_count), BF)
        if last:
            mine = weight.astype(BF)
            sent = mine
            keep = mine.astype(F32)
        else:
            side = (ctx_at // bit) % 2
            two = weight.reshape(2, weight.shape[0] // 2, chan_count)
            sent = pick(two, 1 - side).astype(BF)
            keep = pick(two, side)
            halved.append((bit, side))
        rows = sent.shape[0]
        got = swap(jnp.concatenate([sent, hi, lo, pad], 0), "ctx", bit)
        weight = keep + got[:rows].astype(F32)
        taps_sum = (hi.astype(F32) + lo.astype(F32)) + (
            got[rows : rows + tap_count].astype(F32)
            + got[rows + tap_count : rows + 2 * tap_count].astype(F32)
        )
        bit *= 2
    whole = weight.astype(BF)
    for bit, side in reversed(halved):
        other = swap(whole, "ctx", bit)
        low = jnp.where(side == 0, whole, other)
        high = jnp.where(side == 0, other, whole)
        whole = jnp.concatenate([low, high], 0)
    by_rel = whole.reshape(ch_count, chan_count, chan_count)
    place = {o: k for k, o in enumerate(order)}
    grad_gate_weight = jnp.concatenate(
        [
            pick(by_rel, jnp.array([place[o] for o in range(ch_count)])[ch_at ^ j])
            for j in range(ch_count)
        ],
        0,
    ).astype(F32)

    parts = {
        o: lax.dot_general(grad_gate, w, (((1,), (1,)), ((), ())), preferred_element_type=F32)
        for o, w in zip(order, w_rel)
    }
    bit = 1
    while bit < ch_count:
        merged = {}
        for o in parts:
            if not o & bit:
                merged[o] = parts[o] + swap(parts[o | bit].astype(BF), "ch", bit).astype(F32)
        parts = merged
        bit *= 2
    gate_input_grad = parts[0]

    second_part = jnp.einsum("mrc,nrc->rmn", grad_cols, columns, preferred_element_type=F32)
    grad_first_t = jnp.einsum(
        "rmn,mrc->nrc", block_second, grad_cols, preferred_element_type=F32
    ).astype(BF)
    grad_back = lax.all_to_all(grad_first_t, "ctx", split_axis=0, concat_axis=1, tiled=True)
    grad_second = second_part
    bit = 1
    while bit < ch_count:
        grad_second = grad_second + swap(grad_second, "ch", bit)
        bit *= 2

    first_part = jnp.einsum("nrc,nsc->nrs", grad_back, local_blocks, preferred_element_type=F32)
    grad_local = jnp.einsum(
        "nrs,nrc->nsc", block_first, grad_back, preferred_element_type=F32
    ).reshape(tok_rows, chan_count)
    grad_tokens = (grad_local + gate_input_grad).astype(BF)

    core = ch_at % 2
    split = first_part.reshape(2, -1, block_size)
    mine = (pick(split, core) + swap(pick(split, 1 - core).astype(BF), "ch", 1).astype(F32)).astype(
        BF
    )
    bit = 2
    total = mine.astype(F32)
    while bit < ch_count:
        total = total + swap(total.astype(BF), "ch", bit).astype(F32)
        bit *= 2
    other = swap(total, "ch", 1)
    grad_first = jnp.concatenate(
        [jnp.where(core == 0, total, other), jnp.where(core == 0, other, total)], 0
    ).reshape(first_part.shape)
    return (mixed_out, grad_tokens, taps_sum, grad_gate_weight, grad_first, grad_second)


def solution(mesh):
    in_specs = (
        P("ctx", "ch"),
        P("ctx", None, None),
        P("ctx", None, None),
        P(None, "ch"),
        P(None, "ch"),
        P("ctx", "ch"),
    )
    out_specs = (
        P("ctx", "ch"),
        P("ctx", "ch"),
        P(None, "ch"),
        P(None, "ch"),
        P("ctx", None, None),
        P("ctx", None, None),
    )
    return jax.shard_map(
        on_device, mesh=mesh, in_specs=in_specs, out_specs=out_specs, check_vma=False
    )
```

```python
import functools

import jax
import jax.numpy as jnp
from jax import lax
from jax.experimental import pallas as pl
from jax.experimental.pallas import tpu as pltpu
from jax.sharding import PartitionSpec as P

BF = jnp.bfloat16
F32 = jnp.float32
HALO = 16
PAD = 8


NN = (((1,), (0,)), ((), ()))
NT = (((1,), (1,)), ((), ()))
TN = (((0,), (0,)), ((), ()))


def mm(a, b, dims=NN):
    return lax.dot_general(a, b, dims, preferred_element_type=F32)


def call(body, name, outs, args, flops, scratch=(), scalars=()):
    moved = sum(a.size * a.dtype.itemsize for a in args)
    moved += sum(o.size * o.dtype.itemsize for o in outs)
    vmem = pl.BlockSpec(memory_space=pltpu.VMEM)
    smem = pl.BlockSpec(memory_space=pltpu.SMEM)
    return pl.pallas_call(
        body,
        name=name,
        out_shape=outs,
        in_specs=[smem] * len(scalars) + [vmem] * len(args),
        out_specs=[vmem] * len(outs),
        scratch_shapes=list(scratch),
        cost_estimate=pl.CostEstimate(flops=flops, bytes_accessed=moved, transcendentals=0),
    )(*scalars, *args)


def shape(dims, dtype):
    return jax.ShapeDtypeStruct(dims, dtype)


def passed_along(array, axis, by):
    count = lax.axis_size(axis)
    pairs = [(i, i + by) for i in range(count) if 0 <= i + by < count]
    return lax.ppermute(array, axis, pairs)


def swap(array, axis, bit):
    count = lax.axis_size(axis)
    return lax.ppermute(array, axis, [(i, i ^ bit) for i in range(count)])


def pick(stacked, index):
    return lax.dynamic_index_in_dim(stacked, index, 0, keepdims=False)


def exchange(blocked):
    return lax.all_to_all(blocked, "ctx", split_axis=0, concat_axis=0, tiled=True)


def merged(x, dims):
    if x.dtype == BF and (x.shape[-2] % 16 or dims[-2] % 16):
        return x.astype(F32).reshape(dims).astype(BF)
    return x.reshape(dims)


def first_body(first, tok, out):
    blocks, size, _ = first.shape
    devices, _, rows, chans = out.shape
    for n in range(blocks):
        made = mm(first[n], tok[n * size : (n + 1) * size, :]).astype(BF)
        out[:, n] = merged(made, (devices, rows, chans))


def gate_body(where, t0, t1, t2, t3, weight, cot, after, taps, sig_out, slope_out, wide, mix_out):
    rows, chans = t0.shape
    devices, blocks, part, _ = mix_out.shape
    wide[0:rows, :] = cot[...].astype(F32)
    wide[rows : rows + PAD, :] = after[0:HALO, :].astype(F32)[0:PAD]
    tile = rows // blocks // 2
    tap_count = taps.shape[0]
    for i in range(rows // tile):
        at = i * tile
        pre = jnp.zeros((tile, chans), F32)
        for k, t in enumerate((t0, t1, t2, t3)):
            w = weight[pl.ds(pl.multiple_of((where[0] ^ k) * chans, chans), chans), :]
            pre = pre + mm(t[at : at + tile, :], w)
        sig = jax.nn.sigmoid(pre)
        grad = jnp.zeros((tile, chans), F32)
        for k in range(tap_count):
            grad = grad + taps[k : k + 1, :] * wide[at + k : at + k + tile, :]
        mix = grad * sig
        sig_out[at : at + tile, :] = sig
        slope_out[at : at + tile, :] = mix * (1.0 - sig)
        n, start = at // (rows // blocks), at % (rows // blocks)
        count = tile // part
        mix_out[start // part : start // part + count, n] = merged(
            mix.astype(BF), (count, part, chans)
        )


def gated_body(mixed, sig, slope, wide, gated_out, gate_out, taps_out):
    devices, blocks, part, chans = mixed.shape
    size = devices * part
    tap_count = 4
    sums = [jnp.zeros((1, chans), F32) for _ in range(tap_count)]
    half = devices // 2
    for n in range(blocks):
        for h in range(2):
            at = n * size + h * half * part
            span = half * part
            mix = merged(mixed[h * half : (h + 1) * half, n], (span, chans)).astype(F32)
            gated = (mix * sig[at : at + span, :]).astype(BF)
            gated_out[at : at + span, :] = gated
            gate_out[at : at + span, :] = (mix * slope[at : at + span, :]).astype(BF)
            gated = gated.astype(F32)
            for k in range(tap_count):
                sums[k] = sums[k] + jnp.sum(
                    gated * wide[at + k : at + k + span, :], axis=0, keepdims=True
                )
    for k in range(tap_count):
        taps_out[k : k + 1, :] = sums[k]


def weight_body(t0, t1, t2, t3, grad, out):
    chans = grad.shape[1]
    for k, t in enumerate((t0, t1, t2, t3)):
        out[k * chans : (k + 1) * chans, :] = mm(t[...], grad[...], TN)


def parts_body(where, grad, weight, keep0, keep2, send):
    chans = grad.shape[1]
    for k in range(4):
        w = weight[pl.ds(pl.multiple_of((where[0] ^ k) * chans, chans), chans), :]
        part = mm(grad[...], w, NT)
        if k % 2:
            send[k // 2] = part.astype(BF)
        elif k == 0:
            keep0[...] = part
        else:
            keep2[...] = part


def conv_body(gated, before, taps, out, wide):
    rows, chans = gated.shape
    tap_count = taps.shape[0]
    wide[0:PAD, :] = before[...].astype(F32)[HALO - PAD :]
    wide[PAD : rows + PAD, :] = gated[...].astype(F32)
    tile = rows // 4
    for i in range(4):
        at = i * tile
        total = jnp.zeros((tile, chans), F32)
        for k in range(tap_count):
            total = total + taps[k : k + 1, :] * wide[at + PAD - k : at + PAD - k + tile, :]
        out[at : at + tile, :] = total.astype(BF)


def spread_body(spread, cols, out):
    groups, wide, _ = spread.shape
    count, rows, chans = cols.shape
    per = rows // groups
    for g in range(groups):
        block = merged(cols[:, g * per : (g + 1) * per, :], (wide, chans))
        made = mm(spread[g], block).astype(BF)
        out[:, g * per : (g + 1) * per, :] = merged(made, (count, per, chans))


def back_body(spread, cols, grads, out, second):
    groups, wide, _ = spread.shape
    count, rows, chans = cols.shape
    per = rows // groups
    row = lax.broadcasted_iota(jnp.int32, (wide, wide), 0) % per
    col = lax.broadcasted_iota(jnp.int32, (wide, wide), 1) % per
    same = row == col
    fold = lax.broadcasted_iota(jnp.int32, (count, wide), 1) // per
    fold = (fold == lax.broadcasted_iota(jnp.int32, (count, wide), 0)).astype(F32)
    for g in range(groups):
        span = slice(g * per, (g + 1) * per)
        given = merged(grads[:, span, :], (wide, chans))
        block = merged(cols[:, span, :], (wide, chans))
        made = mm(spread[g], given, TN).astype(BF)
        out[:, span, :] = merged(made, (count, per, chans))
        cross = jnp.where(same, mm(given, block, NT), 0.0)
        second[:, g * wide : (g + 1) * wide] = lax.dot_general(
            fold, cross, NT, preferred_element_type=F32, precision=lax.Precision.HIGHEST
        )


def outer_body(core, back, tok, keep, send):
    devices, blocks, part, chans = back.shape
    size = devices * part
    half = blocks // 2
    for j in range(half):
        for mine in range(2):
            n = (core[0] if mine else 1 - core[0]) * half + j
            grads = merged(back[:, n], (size, chans))
            made = mm(grads, tok[pl.ds(pl.multiple_of(n * size, size), size), :], NT)
            if mine:
                keep[j] = made
            else:
                send[j] = made.astype(BF)


def inner_body(first, back, extra, out):
    blocks, size, _ = first.shape
    devices, _, part, chans = back.shape
    for n in range(blocks):
        grads = merged(back[:, n], (size, chans))
        span = slice(n * size, (n + 1) * size)
        out[span, :] = (mm(first[n], grads, TN) + extra[span, :]).astype(BF)


def on_device(tokens, block_first, block_second, gate_weight, conv_taps, cotangent):
    blocks, block_size, _ = block_first.shape
    rows, chans = tokens.shape
    tap_count = conv_taps.shape[0]
    ctx_count = lax.axis_size("ctx")
    ch_count = lax.axis_size("ch")
    ctx_at = lax.axis_index("ctx")
    ch_at = lax.axis_index("ch")
    total_blocks = block_second.shape[1]
    part = block_second.shape[0]
    where = ch_at.astype(jnp.int32).reshape(1)
    core = (ch_at % 2).astype(jnp.int32).reshape(1)
    blocked = (ctx_count, blocks, part, chans)
    flat = (total_blocks, part, chans)
    flops = 2 * rows * chans * block_size

    with jax.named_scope("agx"):
        t2 = swap(tokens, "ch", 2)
    with jax.named_scope("agc0"):
        t1 = swap(tokens, "ch", 1)
    with jax.named_scope("after"):
        after = passed_along(cotangent[:HALO], "ctx", -1)
    (first_out,) = call(
        first_body, "first", [shape(blocked, BF)], (block_first, tokens), flops
    )
    with jax.named_scope("a2a1"):
        columns = exchange(first_out).reshape(flat)

    per = min(16, part)
    groups = part // per
    wide = total_blocks * per
    rows_of = (
        block_second.reshape(groups, per, total_blocks, total_blocks)
        .transpose(0, 2, 1, 3)
        .reshape(groups * wide, total_blocks)
    )
    lane = lax.broadcasted_iota(jnp.int32, (total_blocks, wide), 1)
    expand = (lane // per == lax.broadcasted_iota(jnp.int32, (total_blocks, wide), 0)).astype(BF)
    row_at = lax.broadcasted_iota(jnp.int32, (groups * wide, wide), 0) % per
    col_at = lax.broadcasted_iota(jnp.int32, (groups * wide, wide), 1) % per
    spread = jnp.where(row_at == col_at, mm(rows_of, expand), 0.0).astype(BF)
    spread = spread.reshape(groups, wide, wide)

    with jax.named_scope("agc1"):
        t3 = swap(t2, "ch", 1)
    feats = (tokens, t1, t2, t3)

    (second_out,) = call(
        spread_body, "mixf", [shape(flat, BF)], (spread, columns), 2 * wide * rows * chans
    )
    with jax.named_scope("a2a2"):
        mixed = exchange(second_out.reshape(blocked))

    sig, slope, cot_wide, grad_mix = call(
        gate_body,
        "gate",
        [
            shape((rows, chans), F32),
            shape((rows, chans), F32),
            shape((rows + PAD, chans), F32),
            shape(blocked, BF),
        ],
        (*feats, gate_weight, cotangent, after, conv_taps),
        2 * rows * chans * chans * ch_count,
        scalars=(where,),
    )
    with jax.named_scope("a2a3"):
        grad_cols = exchange(grad_mix).reshape(flat)

    gated, grad_gate, taps_sum = call(
        gated_body,
        "gated",
        [shape((rows, chans), BF), shape((rows, chans), BF), shape((tap_count, chans), F32)],
        (mixed, sig, slope, cot_wide),
        20 * rows * chans,
    )
    with jax.named_scope("before"):
        before = passed_along(gated[rows - HALO :], "ctx", 1)
    (weight,) = call(
        weight_body,
        "weight",
        [shape((ch_count * chans, chans), F32)],
        (*feats, grad_gate),
        2 * rows * chans * chans * ch_count,
    )
    bits = []
    bit = 1
    while bit < ctx_count:
        bits.append(bit)
        bit *= 2

    def halving(name, whole, order):
        halved = []
        for bit in order[:-1]:
            side = (ctx_at // bit) % 2
            two = whole.reshape(2, whole.shape[0] // 2, chans)
            with jax.named_scope(f"{name}s{bit}"):
                got = swap(pick(two, 1 - side).astype(BF), "ctx", bit)
            whole = pick(two, side) + got.astype(F32)
            halved.append((bit, side))
        mine = whole.astype(BF)
        with jax.named_scope(f"{name}m{order[-1]}"):
            got = swap(mine, "ctx", order[-1])
        whole = (mine.astype(F32) + got.astype(F32)).astype(BF)
        for bit, side in reversed(halved):
            with jax.named_scope(f"{name}g{bit}"):
                other = swap(whole, "ctx", bit)
            low = jnp.where(side == 0, whole, other)
            high = jnp.where(side == 0, other, whole)
            whole = jnp.concatenate([low, high], 0)
        return whole

    near, middle, last = bits[:-2], bits[-2], bits[-1]
    half = weight.shape[0] // 2
    by_rel = jnp.concatenate(
        [
            halving("wa", weight[:half], near + [middle, last]),
            halving("wb", weight[half:], [middle] + near + [last]),
        ],
        0,
    ).reshape(ch_count, chans, chans)
    grad_gate_weight = jnp.concatenate(
        [pick(by_rel, ch_at ^ j) for j in range(ch_count)], 0
    ).astype(F32)

    (mixed_out,) = call(
        conv_body,
        "conv",
        [shape((rows, chans), BF)],
        (gated, before, conv_taps),
        8 * rows * chans,
        scratch=[pltpu.VMEM((rows + PAD, chans), F32)],
    )
    for bit in bits:
        with jax.named_scope(f"taps{bit}"):
            taps_sum = taps_sum + swap(taps_sum, "ctx", bit)

    keep0, keep2, send = call(
        parts_body,
        "parts",
        [
            shape((rows, chans), F32),
            shape((rows, chans), F32),
            shape((2, rows, chans), BF),
        ],
        (grad_gate, gate_weight),
        2 * rows * chans * chans * ch_count,
        scalars=(where,),
    )
    with jax.named_scope("rsc"):
        got = swap(send, "ch", 1)
    with jax.named_scope("rsx"):
        got2 = swap((keep2 + got[1].astype(F32)).astype(BF), "ch", 2)
    extra = keep0 + got[0].astype(F32) + got2.astype(F32)

    grad_first_t, second_part = call(
        back_body,
        "mixb",
        [shape(flat, BF), shape((total_blocks, groups * wide), F32)],
        (spread, columns, grad_cols),
        4 * wide * rows * chans,
    )
    with jax.named_scope("a2a4"):
        back = exchange(grad_first_t.reshape(blocked))
    for bit in (1, 2):
        with jax.named_scope(f"second{bit}"):
            second_part = second_part + swap(second_part, "ch", bit)
    grad_second = (
        second_part.reshape(total_blocks, groups, total_blocks, per)
        .transpose(1, 3, 2, 0)
        .reshape(block_second.shape)
    )

    keep, send = call(
        outer_body,
        "outer",
        [
            shape((blocks // 2, block_size, block_size), F32),
            shape((blocks // 2, block_size, block_size), BF),
        ],
        (back, tokens),
        flops,
        scalars=(core,),
    )
    with jax.named_scope("firstc"):
        got = swap(send, "ch", 1)
    mine = (keep + got.astype(F32)).astype(BF)
    with jax.named_scope("firstx"):
        got = swap(mine, "ch", 2)
    total = mine.astype(F32) + got.astype(F32)
    with jax.named_scope("firstg"):
        other = swap(total, "ch", 1)
    grad_first = jnp.concatenate(
        [jnp.where(core[0] == 0, total, other), jnp.where(core[0] == 0, other, total)], 0
    )
    (grad_tokens,) = call(
        inner_body, "inner", [shape((rows, chans), BF)], (block_first, back, extra), flops
    )
    return (mixed_out, grad_tokens, taps_sum, grad_gate_weight, grad_first, grad_second)


def solution(mesh):
    in_specs = (
        P("ctx", "ch"),
        P("ctx", None, None),
        P("ctx", None, None),
        P(None, "ch"),
        P(None, "ch"),
        P("ctx", "ch"),
    )
    out_specs = (
        P("ctx", "ch"),
        P("ctx", "ch"),
        P(None, "ch"),
        P(None, "ch"),
        P("ctx", None, None),
        P("ctx", None, None),
    )
    return jax.shard_map(
        on_device, mesh=mesh, in_specs=in_specs, out_specs=out_specs, check_vma=False
    )
```

```python
import jax
import jax.numpy as jnp
from jax import lax
from jax.experimental import pallas as pl
from jax.experimental.pallas import tpu as pltpu
from jax.sharding import PartitionSpec as P


BF = jnp.bfloat16
F32 = jnp.float32
HALO = 16
PAD = 8


NN = (((1,), (0,)), ((), ()))
NT = (((1,), (1,)), ((), ()))
TN = (((0,), (0,)), ((), ()))


def mm(a, b, dims=NN):
    return lax.dot_general(a, b, dims, preferred_element_type=F32)


def call(body, outs, args, flops, scratch=(), scalars=()):
    moved = sum(a.size * a.dtype.itemsize for a in args)
    moved += sum(o.size * o.dtype.itemsize for o in outs)
    vmem = pl.BlockSpec(memory_space=pltpu.VMEM)
    smem = pl.BlockSpec(memory_space=pltpu.SMEM)
    return pl.pallas_call(
        body,
        out_shape=outs,
        in_specs=[smem] * len(scalars) + [vmem] * len(args),
        out_specs=[vmem] * len(outs),
        scratch_shapes=list(scratch),
        cost_estimate=pl.CostEstimate(flops=flops, bytes_accessed=moved, transcendentals=0),
    )(*scalars, *args)


def shape(dims, dtype):
    return jax.ShapeDtypeStruct(dims, dtype)


def passed_along(array, axis, by):
    count = lax.axis_size(axis)
    pairs = [(i, i + by) for i in range(count) if 0 <= i + by < count]
    return lax.ppermute(array, axis, pairs)


def swap(array, axis, bit):
    count = lax.axis_size(axis)
    return lax.ppermute(array, axis, [(i, i ^ bit) for i in range(count)])


def pick(stacked, index):
    return lax.dynamic_index_in_dim(stacked, index, 0, keepdims=False)


def exchange(blocked):
    return lax.all_to_all(blocked, "ctx", split_axis=0, concat_axis=0, tiled=True)


def merged(x, dims):
    if x.dtype == BF and (x.shape[-2] % 16 or dims[-2] % 16):
        return x.astype(F32).reshape(dims).astype(BF)
    return x.reshape(dims)


def first_body(first, tok, out):
    blocks, size, _ = first.shape
    devices, _, rows, chans = out.shape
    for n in range(blocks):
        made = mm(first[n], tok[n * size : (n + 1) * size, :]).astype(BF)
        out[:, n] = merged(made, (devices, rows, chans))


def gate_body(where, t0, t1, t2, t3, weight, cot, after, taps, sig_out, slope_out, wide, *rest):
    mix_outs, mix_out = rest[:-1], rest[-1]
    rows, chans = t0.shape
    _, blocks, part, _ = mix_out.shape
    wide[0:rows, :] = cot[...].astype(F32)
    wide[rows : rows + PAD, :] = after[0:HALO, :].astype(F32)[0:PAD]
    tile = rows // blocks // 2
    tap_count = taps.shape[0]
    for i in range(rows // tile):
        at = i * tile
        pre = jnp.zeros((tile, chans), F32)
        for k, t in enumerate((t0, t1, t2, t3)):
            w = weight[pl.ds(pl.multiple_of((where[0] ^ k) * chans, chans), chans), :]
            pre = pre + mm(t[at : at + tile, :], w)
        sig = jax.nn.sigmoid(pre)
        grad = jnp.zeros((tile, chans), F32)
        for k in range(tap_count):
            grad = grad + taps[k : k + 1, :] * wide[at + k : at + k + tile, :]
        mix = grad * sig
        sig_out[at : at + tile, :] = sig
        slope_out[at : at + tile, :] = mix * (1.0 - sig)
        n, start = at // (rows // blocks), at % (rows // blocks)
        count = tile // part
        mix_out[start // part : start // part + count, n] = merged(
            mix.astype(BF), (count, part, chans)
        )
    for k, out in enumerate(mix_outs):
        out[...] = mix_out[where[1] ^ k]


def flip_body(t0, t1, t2, t3, out):
    chans = t0.shape[1]
    for k, t in enumerate((t0, t1, t2, t3)):
        out[k * chans : (k + 1) * chans, :] = t[...].T


def gated_body(mixed, sig, slope, gated_out, gate_out):
    devices, blocks, part, chans = mixed.shape
    half = devices // 2
    span = half * part
    for n in range(blocks):
        for h in range(2):
            at = n * 2 * span + h * span
            mix = merged(mixed[h * half : (h + 1) * half, n], (span, chans)).astype(F32)
            gated_out[at : at + span, :] = (mix * sig[at : at + span, :]).astype(BF)
            gate_out[at : at + span, :] = (mix * slope[at : at + span, :]).astype(BF)


def weight_body(sides, flipped, grad, keep_a, keep_b, send_a, send_b):
    quarter = keep_a.shape[0]
    for which, (keep, send) in enumerate(((keep_a, send_a), (keep_b, send_b))):
        for mine in range(2):
            side = sides[which] if mine else 1 - sides[which]
            at = pl.multiple_of((2 * which + side) * quarter, quarter)
            made = mm(flipped[pl.ds(at, quarter), :], grad[...])
            if mine:
                keep[...] = made
            else:
                send[...] = made.astype(BF)


def parts_body(where, grad, weight, keep0, keep2, send):
    chans = grad.shape[1]
    for k in range(4):
        w = weight[pl.ds(pl.multiple_of((where[0] ^ k) * chans, chans), chans), :]
        part = mm(grad[...], w, NT)
        if k % 2:
            send[k // 2] = part.astype(BF)
        elif k == 0:
            keep0[...] = part
        else:
            keep2[...] = part


def conv_body(gated, before, taps, ahead, out, taps_out, wide):
    rows, chans = gated.shape
    tap_count = taps.shape[0]
    wide[0:PAD, :] = before[...].astype(F32)[HALO - PAD :]
    wide[PAD : rows + PAD, :] = gated[...].astype(F32)
    tile = rows // 4
    sums = [jnp.zeros((1, chans), F32) for _ in range(tap_count)]
    for i in range(4):
        at = i * tile
        total = jnp.zeros((tile, chans), F32)
        here = wide[at + PAD : at + PAD + tile, :]
        for k in range(tap_count):
            total = total + taps[k : k + 1, :] * wide[at + PAD - k : at + PAD - k + tile, :]
            sums[k] = sums[k] + jnp.sum(
                here * ahead[at + k : at + k + tile, :], axis=0, keepdims=True
            )
        out[at : at + tile, :] = total.astype(BF)
    for k in range(tap_count):
        taps_out[k : k + 1, :] = sums[k]


def spread_body(spread, cols, out):
    groups, wide, _ = spread.shape
    count, rows, chans = cols.shape
    per = rows // groups
    for g in range(groups):
        block = merged(cols[:, g * per : (g + 1) * per, :], (wide, chans))
        made = mm(spread[g], block).astype(BF)
        out[:, g * per : (g + 1) * per, :] = merged(made, (count, per, chans))


def back_body(where, spread, cols, *rest):
    given_blocks, (out, second, grads) = rest[:-3], rest[-3:]
    if len(given_blocks) == 1:
        grads[...] = given_blocks[0][...]
    else:
        for k, block in enumerate(given_blocks):
            blocks = block.shape[0]
            grads[pl.ds((where[1] ^ k) * blocks, blocks)] = block[...]
    groups, wide, _ = spread.shape
    count, rows, chans = cols.shape
    per = rows // groups
    row = lax.broadcasted_iota(jnp.int32, (wide, wide), 0) % per
    col = lax.broadcasted_iota(jnp.int32, (wide, wide), 1) % per
    same = row == col
    fold = lax.broadcasted_iota(jnp.int32, (count, wide), 1) // per
    fold = (fold == lax.broadcasted_iota(jnp.int32, (count, wide), 0)).astype(F32)
    for g in range(groups):
        span = slice(g * per, (g + 1) * per)
        given = merged(grads[:, span, :], (wide, chans))
        block = merged(cols[:, span, :], (wide, chans))
        made = mm(spread[g], given, TN).astype(BF)
        out[:, span, :] = merged(made, (count, per, chans))
        cross = jnp.where(same, mm(given, block, NT), 0.0)
        second[:, g * wide : (g + 1) * wide] = lax.dot_general(
            fold, cross, NT, preferred_element_type=F32, precision=lax.Precision.HIGHEST
        )


def outer_body(core, back, tok, keep, send):
    devices, blocks, part, chans = back.shape
    size = devices * part
    half = blocks // 2
    for j in range(half):
        for mine in range(2):
            n = (core[0] if mine else 1 - core[0]) * half + j
            grads = merged(back[:, n], (size, chans))
            made = mm(grads, tok[pl.ds(pl.multiple_of(n * size, size), size), :], NT)
            if mine:
                keep[j] = made
            else:
                send[j] = made.astype(BF)


def inner_body(first, back, keep, near, far, out):
    blocks, size, _ = first.shape
    _, _, _, chans = back.shape
    for n in range(blocks):
        grads = merged(back[:, n], (size, chans))
        span = slice(n * size, (n + 1) * size)
        extra = keep[span, :] + near[0, span, :].astype(F32) + far[span, :].astype(F32)
        out[span, :] = (mm(first[n], grads, TN) + extra).astype(BF)


def layer(tokens, block_first, block_second, gate_weight, conv_taps, cotangent):
    blocks, block_size, _ = block_first.shape
    rows, chans = tokens.shape
    tap_count = conv_taps.shape[0]
    ctx_count = lax.axis_size("ctx")
    ch_count = lax.axis_size("ch")
    ctx_at = lax.axis_index("ctx")
    ch_at = lax.axis_index("ch")
    total_blocks = block_second.shape[1]
    part = block_second.shape[0]
    where = jnp.stack([ch_at, ctx_at]).astype(jnp.int32)
    core = (ch_at % 2).astype(jnp.int32).reshape(1)
    blocked = (ctx_count, blocks, part, chans)
    flat = (total_blocks, part, chans)
    flops = 2 * rows * chans * block_size

    t2 = swap(tokens, "ch", 2)
    t1 = swap(tokens, "ch", 1)
    after = passed_along(cotangent[:HALO], "ctx", -1)
    (first_out,) = call(first_body, [shape(blocked, BF)], (block_first, tokens), flops)
    columns = exchange(first_out).reshape(flat)

    per = min(16, part)
    groups = part // per
    wide = total_blocks * per
    rows_of = (
        block_second.reshape(groups, per, total_blocks, total_blocks)
        .transpose(0, 2, 1, 3)
        .reshape(groups * wide, total_blocks)
    )
    lane = lax.broadcasted_iota(jnp.int32, (total_blocks, wide), 1)
    expand = (lane // per == lax.broadcasted_iota(jnp.int32, (total_blocks, wide), 0)).astype(BF)
    row_at = lax.broadcasted_iota(jnp.int32, (groups * wide, wide), 0) % per
    col_at = lax.broadcasted_iota(jnp.int32, (groups * wide, wide), 1) % per
    spread = jnp.where(row_at == col_at, mm(rows_of, expand), 0.0).astype(BF)
    spread = spread.reshape(groups, wide, wide)

    t3 = swap(t2, "ch", 1)
    feats = (tokens, t1, t2, t3)

    (second_out,) = call(
        spread_body, [shape(flat, BF)], (spread, columns), 2 * wide * rows * chans
    )
    mixed = exchange(second_out.reshape(blocked))

    direct = ctx_count <= 8
    pieces = ctx_count if direct else 0
    sig, slope, cot_wide, *grad_mix = call(
        gate_body,
        [
            shape((rows, chans), F32),
            shape((rows, chans), F32),
            shape((rows + PAD, chans), F32),
        ]
        + [shape(blocked[1:], BF)] * pieces
        + ([] if direct else [shape(blocked, BF)]),
        (*feats, gate_weight, cotangent, after, conv_taps),
        2 * rows * chans * chans * ch_count,
        scratch=[pltpu.VMEM(blocked, BF)] if direct else [],
        scalars=(where,),
    )
    if direct:
        grad_cols = [grad_mix[0]] + [None] * (ctx_count - 1)
        for k in reversed(range(1, ctx_count)):
            grad_cols[k] = swap(grad_mix[k], "ctx", k)
    else:
        grad_cols = [exchange(grad_mix[0]).reshape(flat)]

    (flipped,) = call(
        flip_body, [shape((ch_count * chans, rows), BF)], feats, rows * chans
    )
    gated, grad_gate = call(
        gated_body,
        [shape((rows, chans), BF), shape((rows, chans), BF)],
        (mixed, sig, slope),
        20 * rows * chans,
    )
    before = passed_along(gated[rows - HALO :], "ctx", 1)
    bits = []
    bit = 1
    while bit < ctx_count:
        bits.append(bit)
        bit *= 2

    near, middle, last = bits[:-2], bits[-2], bits[-1]
    order_a, order_b = near + [middle, last], [middle] + near + [last]
    sides = [(ctx_at // order[0]) % 2 for order in (order_a, order_b)]
    quarter = ch_count * chans // 4
    keep_a, keep_b, send_a, send_b = call(
        weight_body,
        [shape((quarter, chans), F32)] * 2 + [shape((quarter, chans), BF)] * 2,
        (flipped, grad_gate),
        2 * rows * chans * chans * ch_count,
        scalars=(jnp.stack(sides).astype(jnp.int32),),
    )

    def halving(kept, sent, order):
        halved = []
        for bit in order[:-1]:
            side = (ctx_at // bit) % 2
            if halved:
                two = kept.reshape(2, kept.shape[0] // 2, chans)
                sent, kept = pick(two, 1 - side).astype(BF), pick(two, side)
            got = swap(sent, "ctx", bit)
            kept = kept + got.astype(F32)
            halved.append((bit, side))
        mine = kept.astype(BF)
        got = swap(mine, "ctx", order[-1])
        whole = (mine.astype(F32) + got.astype(F32)).astype(BF)
        for bit, side in reversed(halved):
            other = swap(whole, "ctx", bit)
            low = jnp.where(side == 0, whole, other)
            high = jnp.where(side == 0, other, whole)
            whole = jnp.concatenate([low, high], 0)
        return whole

    by_rel = jnp.concatenate(
        [halving(keep_a, send_a, order_a), halving(keep_b, send_b, order_b)], 0
    ).reshape(ch_count, chans, chans)
    grad_gate_weight = jnp.concatenate(
        [pick(by_rel, ch_at ^ j) for j in range(ch_count)], 0
    ).astype(F32)

    mixed_out, taps_sum = call(
        conv_body,
        [shape((rows, chans), BF), shape((tap_count, chans), F32)],
        (gated, before, conv_taps, cot_wide),
        8 * rows * chans,
        scratch=[pltpu.VMEM((rows + PAD, chans), F32)],
    )
    for bit in bits:
        taps_sum = taps_sum + swap(taps_sum, "ctx", bit)

    keep0, keep2, send = call(
        parts_body,
        [
            shape((rows, chans), F32),
            shape((rows, chans), F32),
            shape((2, rows, chans), BF),
        ],
        (grad_gate, gate_weight),
        2 * rows * chans * chans * ch_count,
        scalars=(where,),
    )
    got = swap(send, "ch", 1)
    got2 = swap((keep2 + got[1].astype(F32)).astype(BF), "ch", 2)
    near_part, far_part = got, got2

    grad_first_t, second_part = call(
        back_body,
        [shape(flat, BF), shape((total_blocks, groups * wide), F32)],
        (spread, columns, *grad_cols),
        4 * wide * rows * chans,
        scratch=[pltpu.VMEM(flat, BF)],
        scalars=(where,),
    )
    back = exchange(grad_first_t.reshape(blocked))
    for bit in (1, 2):
        second_part = second_part + swap(second_part, "ch", bit)
    grad_second = (
        second_part.reshape(total_blocks, groups, total_blocks, per)
        .transpose(1, 3, 2, 0)
        .reshape(block_second.shape)
    )

    keep, send = call(
        outer_body,
        [
            shape((blocks // 2, block_size, block_size), F32),
            shape((blocks // 2, block_size, block_size), BF),
        ],
        (back, tokens),
        flops,
        scalars=(core,),
    )
    got = swap(send, "ch", 1)
    mine = (keep + got.astype(F32)).astype(BF)
    got = swap(mine, "ch", 2)
    total = mine.astype(F32) + got.astype(F32)
    other = swap(total, "ch", 1)
    grad_first = jnp.concatenate(
        [jnp.where(core[0] == 0, total, other), jnp.where(core[0] == 0, other, total)], 0
    )
    (grad_tokens,) = call(
        inner_body,
        [shape((rows, chans), BF)],
        (block_first, back, keep0, near_part, far_part),
        flops,
    )
    return (mixed_out, grad_tokens, taps_sum, grad_gate_weight, grad_first, grad_second)


def solution(mesh):
    in_specs = (
        P("ctx", "ch"),
        P("ctx", None, None),
        P("ctx", None, None),
        P(None, "ch"),
        P(None, "ch"),
        P("ctx", "ch"),
    )
    out_specs = (
        P("ctx", "ch"),
        P("ctx", "ch"),
        P(None, "ch"),
        P(None, "ch"),
        P("ctx", None, None),
        P("ctx", None, None),
    )
    return jax.shard_map(
        layer, mesh=mesh, in_specs=in_specs, out_specs=out_specs, check_vma=False
    )
```
